32 devices in a mesh: dp: 4 (over x, core), expert: 8 (over z, y).
Axes of the slice: x: 2, y: 2, z: 4, core: 2. Of those that a mesh axis runs over, the one named last changes fastest.
Arguments:
- hidden_in: bfloat16 [8192, 1024], P(('dp', 'expert')), may hold values from -6 to 6
- d_out: bfloat16 [8192, 1024], P(('dp', 'expert')), may hold values from -6 to 6
- gain_attn: bfloat16 [1024], P('dp'), may hold values from 0.25 to 1.75
- w_qkv: bfloat16 [1024, 2048], P('dp'), may hold values from -0.1875 to 0.1875
- w_o: bfloat16 [1024, 1024], P('dp'), may hold values from -1.5 to 1.5
- gain_moe: bfloat16 [1024], P('dp'), may hold values from 0.25 to 1.75
- w_router: bfloat16 [1024, 16], P('dp'), may hold values from -0.375 to 0.375
- w_in: bfloat16 [16, 1024, 1024], P('expert', 'dp'), may hold values from -0.1875 to 0.1875
- w_out: bfloat16 [16, 512, 1024], P('expert', None, 'dp'), may hold values from -0.75 to 0.75
- seq_lengths: int32 [4, 4], P('dp'), may hold values from 1 to 1024, 2048 in all within a row
- assign: int32 [4, 2048], P('dp', 'expert'), may hold values from 0 to 2047, each once within a row
- routes: int32 [8192, 8], P(('dp', 'expert')), may hold values from 0 to 15, all different within a row; in each aligned block of 256 rows (0 to 255, 256 to 511, ...) at most 192 rows name the same one
Outputs:
- layer_out: bfloat16 [8192, 1024], P(('dp', 'expert'))
- grad_in: float32 [8192, 1024], P(('dp', 'expert'))
- grad_gain_attn: float32 [1024], P('dp')
- grad_w_qkv: float32 [1024, 2048], P('dp')
- grad_w_o: float32 [1024, 1024], P('dp')
- grad_gain_moe: float32 [1024], P('dp')
- grad_w_router: float32 [1024, 16], P('dp')
- grad_w_in: float32 [16, 1024, 1024], P('expert', 'dp')
- grad_w_out: float32 [16, 512, 1024], P('expert', None, 'dp')
The draws below stay inside these ranges and needn't reach their ends.
Inputs may be any that keep to these rules, and one draw needn't show every extreme that they name: `assign`: each row of a batch group's stream positions names every position of the group once. `seq_lengths`: each row holds 4 lengths that sum to 2048; the longest is 1024. `routes`: A token names 8 different experts. Within the rows of one device no expert is named by more than 192 rows, and in every draw some device has an expert named by exactly 192 of its rows.
All inputs are finite; a program needn't handle non-finite values.
Results may differ from the reference program's by a relative error of at most 0.015.
Values may be sent and summed in bfloat16 or wider, within the bound.
A program may use at most 192 MiB of HBM per device.

```python
import math
import jax
import jax.numpy as jnp
import numpy as np
from jax import lax

D = 1024
HEADS = 16
KV_HEADS = 8
HEAD_DIM = 64
FF = 512
TOP = 8
NSEQ = 4
SEQ_MAX = 1024
EXPERTS = 16
GROUP_TOK = 2048
TOK_DEV = 256
TOKENS = 8192
CAP = 192
N_DP = 4
DEVICES = 32


def block_scale(key, extent, cuts, low, top_value):
    level = 1.0
    for position, shards_of in cuts:
        steps = jax.random.uniform(jax.random.fold_in(jax.random.fold_in(key, 6), position), (shards_of,), jnp.float32, low / len(cuts), top_value / len(cuts))
        level = level * jnp.repeat(jnp.exp(steps), extent[position] // shards_of).reshape((-1,) + (1,) * (len(extent) - 1 - position))
    return level


def length_profile(number_of, total, limit, lean):
    loads = [(1 << 20) // math.isqrt(standing ** lean) + 1 for standing in range(2, number_of + 1)]
    surplus, given = total - limit - (number_of - 1), [1] * (number_of - 1)
    while surplus > 0:
        candidates = [i for i in range(number_of - 1) if given[i] < limit]
        pool, budget = sum([loads[i] for i in candidates]), surplus
        for i in candidates:
            more = min(limit - given[i], max(1, budget * loads[i] // pool), surplus)
            given[i] = given[i] + more
            surplus = surplus - more
    return np.array([limit] + given)


def ragged(stream_key, count, total, most, slope):
    if count == 2:
        one = jax.random.randint(stream_key, (), max(1, total - most), min(most, total - 1) + 1)
        return jnp.stack([one, total - one])
    lengths = jnp.asarray(length_profile(count, total, most, slope), jnp.int32)
    pairs = (count - 1) // 2
    donor, taker = lengths[1:1 + 2 * pairs:2], lengths[2:2 + 2 * pairs:2]
    slack = jnp.minimum(donor - 1, most - taker)
    shifted = jax.random.randint(jax.random.fold_in(stream_key, 1), (pairs,), 0, 1 << 20) % (slack + 1)
    lengths = lengths.at[1:1 + 2 * pairs:2].set(donor - shifted).at[2:2 + 2 * pairs:2].set(taker + shifted)
    return lengths[jax.random.permutation(jax.random.fold_in(stream_key, 2), count)]


def deal_out(rng, own, number, rows, count, top, most, lean):
    order = jax.random.permutation(rng, count)
    packed, common = load_shares(count, rows * top, most, lean, True), load_shares(count, rows * top, most, lean, False)
    places = jnp.arange(count)

    def named(sizes, offset_by):
        used = int((sizes > 0).sum())
        fixed = max(1, used // 4)
        shifted = fixed + (places - fixed + offset_by * (used - fixed)) % max(1, count - fixed)
        return jnp.zeros((count,), jnp.int32).at[order[jnp.where(places < fixed, places, shifted)]].set(jnp.asarray(sizes, jnp.int32))

    sizes = jnp.where(number % 4 == 0, named(packed, number // 4), named(common, number - number // 4 - 1))
    mixed = jax.random.permutation(jax.random.fold_in(own, 3), count)
    donor, receiver = mixed[0:count // 2 * 2:2], mixed[1:count // 2 * 2:2]
    slack = jnp.minimum(sizes[donor] - 1, most - sizes[receiver]) // 2
    slack = jnp.where((donor == order[0]) | (receiver == order[0]) | (sizes[receiver] == 0), 0, jnp.maximum(slack, 0))
    shifted = jax.random.randint(jax.random.fold_in(own, 4), (count // 2,), 0, 1 << 20) % (slack + 1)
    sizes = sizes.at[donor].add(-shifted).at[receiver].add(shifted)
    items = jnp.searchsorted(jnp.cumsum(sizes), jnp.arange(rows * top), side="right").astype(jnp.int32)
    grid = items.reshape(top, rows).T
    grid = grid[jax.random.permutation(jax.random.fold_in(own, 1), rows)]
    offset_by = jax.random.randint(jax.random.fold_in(own, 2), (rows, 1), 0, top)
    return jnp.take_along_axis(grid, (jnp.arange(top)[None, :] + offset_by) % top, axis=1)


def load_shares(number_of, total, reach, lean, full):
    portions = [(1 << 20) // math.isqrt(rank ** lean) + 1 for rank in range(1, number_of + 1)]
    largest = reach if full else min(reach, max(-(-total // number_of), total * portions[0] // sum(portions)))
    least = 1 if total - largest >= number_of - 1 else 0
    holding, surplus = [largest] + [least] * (number_of - 1), total - largest - least * (number_of - 1)
    while surplus > 0:
        candidates = [i for i in range(1, number_of) if holding[i] < largest] or [i for i in range(1, number_of) if holding[i] < reach]
        mass, left = sum([portions[i] for i in candidates]), surplus
        for i in candidates:
            addition = min(reach - holding[i], max(1, left * portions[i] // mass), surplus)
            holding[i] = holding[i] + addition
            surplus = surplus - addition
    return np.array(holding)


def scatter_about(rng, dims, deviation, reach, cuts=(), kind=jnp.bfloat16):
    drawn = deviation * jax.random.normal(rng, dims, jnp.float32)
    if cuts:
        drawn = drawn * block_scale(rng, dims, cuts, -0.22, 0.18)
    return jnp.clip(drawn, -reach, reach).astype(kind)


def setup_inputs(seed: int = 0) -> dict:
    key_of = jax.random.split(jax.random.key(seed), 13)
    hidden_in = scatter_about(key_of[0], (TOKENS, D), 1.0, 6.0, ((0, 32),))
    d_out = scatter_about(key_of[1], (TOKENS, D), 1.0, 6.0, ((0, 32),))
    gain_attn = jnp.clip(1.0 + 0.15 * jax.random.normal(key_of[2], (D,), jnp.float32), 0.25, 1.75).astype(jnp.bfloat16)
    w_qkv = scatter_about(key_of[3], (D, (HEADS + 2 * KV_HEADS) * HEAD_DIM), D ** -0.5, 0.1875, ((0, 4),))
    w_o = scatter_about(key_of[4], (HEADS * HEAD_DIM, D), 16 ** -0.5, 1.5, ((0, 4),))
    gain_moe = jnp.clip(1.0 + 0.15 * jax.random.normal(key_of[5], (D,), jnp.float32), 0.25, 1.75).astype(jnp.bfloat16)
    w_router = scatter_about(key_of[6], (D, EXPERTS), (D // 4) ** -0.5, 0.375, ((0, 4),))
    w_in = scatter_about(key_of[7], (EXPERTS, D, 2 * FF), D ** -0.5, 0.1875, ((0, 8), (1, 4)))
    w_out = scatter_about(key_of[8], (EXPERTS, FF, D), (FF // 8) ** -0.5, 0.75, ((0, 8), (2, 4)))
    seq_lengths = jax.vmap(lambda own: ragged(own, NSEQ, GROUP_TOK, SEQ_MAX, 2))(jax.random.split(key_of[9], N_DP)).reshape((N_DP, NSEQ)).astype(jnp.int32)
    assign = jax.vmap(lambda own: jax.random.permutation(own, GROUP_TOK))(jax.random.split(key_of[10], N_DP)).reshape((N_DP, GROUP_TOK)).astype(jnp.int32)
    routes_keys = jax.random.split(jax.random.fold_in(key_of[11], 1), TOKENS // TOK_DEV)
    routes_turns = jax.random.permutation(jax.random.fold_in(key_of[11], 3), TOKENS // TOK_DEV)
    routes = jax.vmap(lambda own, number: deal_out(jax.random.fold_in(key_of[11], 2), own, number, TOK_DEV, EXPERTS, TOP, CAP, 1))(routes_keys, routes_turns).reshape((TOKENS, TOP))
    return {"hidden_in": hidden_in, "d_out": d_out, "gain_attn": gain_attn, "w_qkv": w_qkv, "w_o": w_o, "gain_moe": gain_moe, "w_router": w_router, "w_in": w_in, "w_out": w_out, "seq_lengths": seq_lengths, "assign": assign, "routes": routes}


EPSILON = 1e-06
ROPE_BASE = 10000.0
SCORE_SCALE = 0.015625
MASKED = -1e+30

def rms_norm(values, gain_vec):
    factor = lax.rsqrt(lax.optimization_barrier(jnp.mean(values * values, axis=-1, keepdims=True)) + EPSILON)
    return values * factor * gain_vec

def rounded(values):
    return lax.optimization_barrier(values.astype(jnp.bfloat16))

def rotary_tables(positions):
    half_dim = HEAD_DIM // 2
    exponent = jnp.arange(half_dim).astype(jnp.float32) * (2.0 / HEAD_DIM)
    frequency = ROPE_BASE ** (-exponent)
    angles = positions.astype(jnp.float32)[:, None] * frequency[None, :]
    angles = jnp.concatenate([angles, angles], axis=1)
    return (jnp.cos(angles), jnp.sin(angles))

def rotate(values, cosine_tab, sine_tab):
    half_dim = HEAD_DIM // 2
    turned = jnp.concatenate([-values[..., half_dim:], values[..., :half_dim]], axis=-1)
    return values * cosine_tab[:, None, :] + turned * sine_tab[:, None, :]

def rotate_back(grads, cosine_tab, sine_tab):
    half_dim = HEAD_DIM // 2
    scaled = grads * sine_tab[:, None, :]
    turned = jnp.concatenate([scaled[..., half_dim:], -scaled[..., :half_dim]], axis=-1)
    return grads * cosine_tab[:, None, :] + turned

def stream_info(assigned, seq_lengths):
    seq_ends = jnp.cumsum(seq_lengths).astype(jnp.int32)
    seq_starts = seq_ends - seq_lengths
    seq_id = lax.optimization_barrier(jnp.sum((assigned[:, None] >= seq_ends[None, :]).astype(jnp.int32), axis=1))
    matches = seq_id[:, None] == jnp.arange(seq_lengths.shape[0], dtype=jnp.int32)[None, :]
    start_of = lax.optimization_barrier(jnp.sum(jnp.where(matches, seq_starts[None, :], 0), axis=1))
    return (seq_id, assigned - start_of)

def gate_up_grad(gate_pre, up_pre, d_hidden):
    sigmoid = jax.nn.sigmoid(gate_pre)
    activated = gate_pre * sigmoid
    d_gate = d_hidden * up_pre * sigmoid * (1.0 + gate_pre * (1.0 - sigmoid))
    return jnp.concatenate([d_gate, d_hidden * activated], axis=-1)

def masked_scores(query_blk, key_grp, query_pos, query_seg, key_pos, key_seg):
    scores = jnp.einsum('tgrd,kgd->tgrk', query_blk.astype(jnp.float32), key_grp.astype(jnp.float32)) * SCORE_SCALE
    allowed = (query_seg[:, None] == key_seg[None, :]) & (key_pos[None, :] <= query_pos[:, None])
    return jnp.where(allowed[:, None, None, :], scores, MASKED)

def group_forward(query_grp, key_grp, value_grp, positions, segments):
    query_block = min(512, GROUP_TOK)
    block_count = GROUP_TOK // query_block
    groups = HEADS // KV_HEADS
    value_wide = value_grp.astype(jnp.float32)

    def one_block(inputs):
        query_blk, block_pos, block_seg = inputs
        scores = masked_scores(query_blk, key_grp, block_pos, block_seg, positions, segments)
        row_max = lax.optimization_barrier(jnp.max(scores, axis=-1))
        log_total = row_max + jnp.log(lax.optimization_barrier(jnp.sum(jnp.exp(scores - row_max[..., None]), axis=-1)))
        soft_weights = rounded(jnp.exp(scores - log_total[..., None])).astype(jnp.float32)
        attended = jnp.einsum('tgrk,kgd->tgrd', soft_weights, value_wide).astype(jnp.bfloat16)
        return (attended, log_total)
    attended, log_total = lax.map(one_block, (query_grp.reshape(block_count, query_block, KV_HEADS, groups, HEAD_DIM), positions.reshape(block_count, query_block), segments.reshape(block_count, query_block)))
    return (attended.reshape(GROUP_TOK, KV_HEADS, groups, HEAD_DIM), log_total.reshape(GROUP_TOK, KV_HEADS, groups))

def group_backward(query_grp, key_grp, value_grp, positions, segments, attended, log_total, d_attended):
    query_block = min(512, GROUP_TOK)
    block_count = GROUP_TOK // query_block
    groups = HEADS // KV_HEADS
    key_wide = key_grp.astype(jnp.float32)
    value_wide = value_grp.astype(jnp.float32)

    def one_block(running, inputs):
        key_acc, value_acc = running
        query_blk, block_pos, block_seg, attended_blk, total_blk, grad_blk = inputs
        scores = masked_scores(query_blk, key_grp, block_pos, block_seg, positions, segments)
        soft_exact = jnp.exp(scores - total_blk[..., None])
        soft_round = rounded(soft_exact).astype(jnp.float32)
        grad_wide = grad_blk.astype(jnp.float32)
        row_delta = lax.optimization_barrier(jnp.sum(grad_wide * attended_blk.astype(jnp.float32), axis=-1))
        d_soft = jnp.einsum('tgrd,kgd->tgrk', grad_wide, value_wide)
        d_scores = rounded(soft_exact * (d_soft - row_delta[..., None])).astype(jnp.float32)
        d_query = jnp.einsum('tgrk,kgd->tgrd', d_scores, key_wide) * SCORE_SCALE
        key_acc = key_acc + jnp.einsum('tgrk,tgrd->kgd', d_scores, query_blk.astype(jnp.float32)) * SCORE_SCALE
        value_acc = value_acc + jnp.einsum('tgrk,tgrd->kgd', soft_round, grad_wide)
        return ((key_acc, value_acc), d_query)
    start_acc = jnp.zeros((GROUP_TOK, KV_HEADS, HEAD_DIM), jnp.float32)
    shape_q = (block_count, query_block, KV_HEADS, groups, HEAD_DIM)
    (key_acc, value_acc), d_query = lax.scan(one_block, (start_acc, start_acc), (query_grp.reshape(shape_q), positions.reshape(block_count, query_block), segments.reshape(block_count, query_block), attended.reshape(shape_q), log_total.reshape(block_count, query_block, KV_HEADS, groups), d_attended.reshape(shape_q)))
    return (d_query.reshape(GROUP_TOK, HEADS, HEAD_DIM), key_acc, value_acc)

def reference(hidden_in, d_out, gain_attn, w_qkv, w_o, gain_moe, w_router, w_in, w_out, seq_lengths, assign, routes):
    groups = HEADS // KV_HEADS
    q_cols = HEADS * HEAD_DIM
    k_cols = KV_HEADS * HEAD_DIM
    stream_in = hidden_in.astype(jnp.float32)
    gain_one = gain_attn.astype(jnp.float32)
    gain_two = gain_moe.astype(jnp.float32)
    normed_one = rms_norm(stream_in, gain_one).astype(jnp.bfloat16)
    projected = jnp.dot(normed_one, w_qkv, preferred_element_type=jnp.float32)
    segments, rot_pos = jax.vmap(stream_info)(assign, seq_lengths)
    cosine_tab, sine_tab = rotary_tables(rot_pos.reshape(TOKENS))
    query_rot = rotate(projected[:, :q_cols].reshape(TOKENS, HEADS, HEAD_DIM), cosine_tab, sine_tab).astype(jnp.bfloat16)
    key_rot = rotate(projected[:, q_cols:q_cols + k_cols].reshape(TOKENS, KV_HEADS, HEAD_DIM), cosine_tab, sine_tab).astype(jnp.bfloat16)
    value_all = projected[:, q_cols + k_cols:].astype(jnp.bfloat16).reshape(TOKENS, KV_HEADS, HEAD_DIM)
    shape_q = (N_DP, GROUP_TOK, KV_HEADS, groups, HEAD_DIM)
    shape_k = (N_DP, GROUP_TOK, KV_HEADS, HEAD_DIM)
    query_groups = query_rot.reshape(shape_q)
    key_groups = key_rot.reshape(shape_k)
    value_groups = value_all.reshape(shape_k)

    def forward_group(inputs):
        return group_forward(*inputs)
    attended, log_total = lax.map(forward_group, (query_groups, key_groups, value_groups, assign, segments))
    attended_flat = attended.reshape(TOKENS, q_cols)
    mid_stream = stream_in + jnp.dot(attended_flat, w_o, preferred_element_type=jnp.float32)
    normed_two = rms_norm(mid_stream, gain_two).astype(jnp.bfloat16)
    logits = jnp.dot(normed_two, w_router, preferred_element_type=jnp.float32)
    gate_probs = jax.nn.softmax(jnp.take_along_axis(logits, routes, axis=1), axis=1)
    route_hits = (routes[:, :, None] == jnp.arange(EXPERTS, dtype=jnp.int32)[None, None, :]).astype(jnp.int32)
    per_row = lax.optimization_barrier(jnp.sum(route_hits, axis=1)).reshape(DEVICES, TOK_DEV, EXPERTS)
    before = (jnp.cumsum(per_row, axis=1) - per_row).reshape(TOKENS, EXPERTS)
    slot_of = lax.optimization_barrier(jnp.sum(route_hits * before[:, None, :], axis=2))
    rows_per = DEVICES * CAP
    device_of = (jnp.arange(TOKENS, dtype=jnp.int32) // TOK_DEV)[:, None]
    target = (routes * rows_per + device_of * CAP + slot_of).reshape(-1)
    token_of = jnp.broadcast_to(jnp.arange(TOKENS, dtype=jnp.int32)[:, None], (TOKENS, TOP)).reshape(-1)
    row_table = jnp.full((EXPERTS * rows_per,), TOKENS, jnp.int32).at[target].set(token_of).reshape(EXPERTS, rows_per)
    gate_table = jnp.zeros((EXPERTS * rows_per,), jnp.float32).at[target].set(gate_probs.reshape(-1)).reshape(EXPERTS, rows_per)
    normed_pad = jnp.concatenate([normed_two, jnp.zeros((1, D), jnp.bfloat16)], axis=0)
    cotangent = d_out.astype(jnp.float32)
    cotangent_pad = jnp.concatenate([cotangent, jnp.zeros((1, D), jnp.float32)], axis=0)

    def expert_step(running, inputs):
        moe_acc, back_acc = running
        row_ids, gate_rows, weight_in, weight_out = inputs
        rows_in = normed_pad[row_ids]
        gate_up = jnp.dot(rows_in, weight_in, preferred_element_type=jnp.float32)
        gate_pre = gate_up[:, :FF]
        up_pre = gate_up[:, FF:]
        hidden = (jax.nn.silu(gate_pre) * up_pre).astype(jnp.bfloat16)
        expert_y = rounded(jnp.dot(hidden, weight_out, preferred_element_type=jnp.float32)).astype(jnp.float32)
        moe_acc = moe_acc.at[row_ids].add(gate_rows[:, None] * expert_y)
        cot_rows = cotangent_pad[row_ids]
        d_gate_rows = lax.optimization_barrier(jnp.sum(cot_rows * expert_y, axis=1))
        d_y = (gate_rows[:, None] * cot_rows).astype(jnp.bfloat16)
        d_hidden = jnp.dot(d_y, weight_out.T, preferred_element_type=jnp.float32)
        grad_out_e = jnp.dot(hidden.T, d_y, preferred_element_type=jnp.float32)
        d_gate_up = gate_up_grad(gate_pre, up_pre, d_hidden).astype(jnp.bfloat16)
        grad_in_e = jnp.dot(rows_in.T, d_gate_up, preferred_element_type=jnp.float32)
        d_slot = rounded(jnp.dot(d_gate_up, weight_in.T, preferred_element_type=jnp.float32)).astype(jnp.float32)
        back_acc = back_acc.at[row_ids].add(d_slot)
        return ((moe_acc, back_acc), (d_gate_rows, grad_in_e, grad_out_e))
    zeros_pad = jnp.zeros((TOKENS + 1, D), jnp.float32)
    (moe_acc, back_acc), (d_gate_tab, grad_w_in, grad_w_out) = lax.scan(expert_step, (zeros_pad, zeros_pad), (row_table, gate_table, w_in, w_out))
    layer_out = (mid_stream + moe_acc[:TOKENS]).astype(jnp.bfloat16)
    d_gate = d_gate_tab.reshape(-1)[target].reshape(TOKENS, TOP)
    d_chosen = gate_probs * (d_gate - lax.optimization_barrier(jnp.sum(gate_probs * d_gate, axis=1, keepdims=True)))
    d_logits = rounded(jnp.einsum('tj,tje->te', d_chosen, route_hits.astype(jnp.float32)))
    grad_w_router = jnp.dot(normed_two.T, d_logits, preferred_element_type=jnp.float32)
    d_normed_two = back_acc[:TOKENS] + jnp.dot(d_logits, w_router.T, preferred_element_type=jnp.float32)
    norm_two_out, norm_two_back = jax.vjp(rms_norm, mid_stream, gain_two)
    d_mid_norm, grad_gain_moe = norm_two_back(d_normed_two)
    d_mid = cotangent + d_mid_norm
    d_attn = d_mid.astype(jnp.bfloat16)
    grad_w_o = jnp.dot(attended_flat.T, d_attn, preferred_element_type=jnp.float32)
    d_attended = jnp.dot(d_attn, w_o.T, preferred_element_type=jnp.float32).astype(jnp.bfloat16)

    def backward_group(inputs):
        return group_backward(*inputs)
    d_query, d_key, d_value = lax.map(backward_group, (query_groups, key_groups, value_groups, assign, segments, attended, log_total, d_attended.reshape(shape_q)))
    dq_pre = rotate_back(d_query.reshape(TOKENS, HEADS, HEAD_DIM), cosine_tab, sine_tab)
    dk_pre = rotate_back(d_key.reshape(TOKENS, KV_HEADS, HEAD_DIM), cosine_tab, sine_tab)
    d_projected = jnp.concatenate([dq_pre.reshape(TOKENS, q_cols), dk_pre.reshape(TOKENS, k_cols), d_value.reshape(TOKENS, k_cols)], axis=1).astype(jnp.bfloat16)
    grad_w_qkv = jnp.dot(normed_one.T, d_projected, preferred_element_type=jnp.float32)
    d_normed_one = jnp.dot(d_projected, w_qkv.T, preferred_element_type=jnp.float32)
    norm_one_out, norm_one_back = jax.vjp(rms_norm, stream_in, gain_one)
    d_in_norm, grad_gain_attn = norm_one_back(d_normed_one)
    grad_in = d_mid + d_in_norm
    return (layer_out, grad_in, grad_gain_attn, grad_w_qkv, grad_w_o, grad_gain_moe, grad_w_router, grad_w_in, grad_w_out)
```

```python
import jax
import jax.numpy as jnp
from jax import lax
from jax.experimental import pallas as pl
from jax.experimental.pallas import tpu as pltpu
from jax.sharding import PartitionSpec as P

HEADS = 16
KV_HEADS = 8
HEAD_DIM = 64
GROUPS = HEADS // KV_HEADS
EPSILON = 1e-06
ROPE_BASE = 10000.0
SCORE_SCALE = 0.015625
MASKED = -1e30
F32 = jnp.float32
BF16 = jnp.bfloat16
Q_TILE = 256
K_TILE = 256


def rms_norm(values, gain_vec):
    factor = lax.rsqrt(jnp.mean(values * values, axis=-1, keepdims=True) + EPSILON)
    return values * factor * gain_vec


def dot(left, right, left_dim=1, right_dim=0):
    return lax.dot_general(
        left, right, (((left_dim,), (right_dim,)), ((), ())), preferred_element_type=F32
    )


def rotate(values, cosine, sine):
    half = HEAD_DIM // 2
    one, two = values[:half], values[half:]
    return jnp.concatenate([one * cosine - two * sine, two * cosine + one * sine], axis=0)


def rotate_back(grads, cosine, sine):
    half = HEAD_DIM // 2
    one, two = grads[:half], grads[half:]
    return jnp.concatenate([one * cosine + two * sine, two * cosine - one * sine], axis=0)


def attend_kernel(low, high, key_pos, query, key, value_t, out, lse, score_buf, weight_buf):
    heads = query.shape[0]
    low_row, high_row = low[...], high[...]
    steps = key.shape[0] // K_TILE

    def score_step(step, maxima):
        rows = pl.ds(pl.multiple_of(step * K_TILE, K_TILE), K_TILE)
        at = key_pos[rows, :]
        allowed = (at >= low_row) & (at <= high_row)
        found = []
        for head in range(heads):
            scores = jnp.dot(key[rows, :], query[head], preferred_element_type=F32)
            scores = jnp.where(allowed, scores, MASKED)
            score_buf[head, rows, :] = scores
            found.append(jnp.maximum(maxima[head], jnp.max(scores, axis=0, keepdims=True)))
        return tuple(found)

    start = tuple(jnp.full(low_row.shape, MASKED, F32) for _ in range(heads))
    maxima = lax.fori_loop(0, steps, score_step, start)

    def weight_step(step, totals):
        rows = pl.ds(pl.multiple_of(step * K_TILE, K_TILE), K_TILE)
        found = []
        for head in range(heads):
            weights = jnp.exp(score_buf[head, rows, :] - maxima[head])
            weight_buf[head, rows, :] = weights.astype(BF16)
            found.append(totals[head] + jnp.sum(weights, axis=0, keepdims=True))
        return tuple(found)

    start = tuple(jnp.zeros(low_row.shape, F32) for _ in range(heads))
    totals = lax.fori_loop(0, steps, weight_step, start)
    for head in range(heads):
        summed = jnp.dot(value_t[...], weight_buf[head], preferred_element_type=F32)
        out[head] = (summed / totals[head]).astype(BF16)
        lse[head] = maxima[head] + jnp.log(totals[head])


def attend(low, high, key_pos, query, key, value_t):
    heads, width, rows = query.shape
    tile = low_tile(rows)
    whole = lambda i: (0, 0)
    lane = lambda i: (0, i)
    return pl.pallas_call(
        attend_kernel,
        grid=(rows // tile,),
        in_specs=[
            pl.BlockSpec((1, tile), lane),
            pl.BlockSpec((1, tile), lane),
            pl.BlockSpec((rows, tile), whole),
            pl.BlockSpec((heads, width, tile), lambda i: (0, 0, i)),
            pl.BlockSpec((rows, width), whole),
            pl.BlockSpec((width, rows), whole),
        ],
        out_specs=[
            pl.BlockSpec((heads, width, tile), lambda i: (0, 0, i)),
            pl.BlockSpec((heads, 1, tile), lambda i: (0, 0, i)),
        ],
        out_shape=[
            jax.ShapeDtypeStruct((heads, width, rows), BF16),
            jax.ShapeDtypeStruct((heads, 1, rows), F32),
        ],
        scratch_shapes=[
            pltpu.VMEM((heads, rows, tile), F32),
            pltpu.VMEM((heads, rows, tile), BF16),
        ],
        cost_estimate=pl.CostEstimate(
            flops=4 * heads * rows * rows * 256,
            bytes_accessed=8 * rows * 256,
            transcendentals=heads * rows * rows,
        ),
        name="attend",
    )(low, high, key_pos, query, key, value_t)


def low_tile(rows):
    return min(Q_TILE, rows)


def attend_back_kernel(
    low, high, key_pos, query, query_n, key, key_t, value, grad, grad_n, lse, delta,
    d_query, d_key, d_value, score_buf,
):
    heads = query.shape[0]
    low_row, high_row = low[...], high[...]
    steps = key.shape[0] // K_TILE

    @pl.when(pl.program_id(0) == 0)
    def _():
        d_key[...] = jnp.zeros_like(d_key)
        d_value[...] = jnp.zeros_like(d_value)

    @pl.loop(0, steps)
    def _(step):
        rows = pl.ds(pl.multiple_of(step * K_TILE, K_TILE), K_TILE)
        at = key_pos[rows, :]
        allowed = (at >= low_row) & (at <= high_row)
        key_sum, value_sum = d_key[rows, :], d_value[rows, :]
        for head in range(heads):
            scores = jnp.dot(key[rows, :], query[head], preferred_element_type=F32)
            weights = jnp.exp(jnp.where(allowed, scores - lse[head], MASKED))
            d_soft = jnp.dot(value[rows, :], grad[head], preferred_element_type=F32)
            d_scores = (weights * (d_soft - delta[head])).astype(BF16)
            score_buf[head, rows, :] = d_scores
            key_sum += jnp.dot(d_scores, query_n[head], preferred_element_type=F32)
            value_sum += jnp.dot(weights.astype(BF16), grad_n[head], preferred_element_type=F32)
        d_key[rows, :] = key_sum
        d_value[rows, :] = value_sum

    for head in range(heads):
        d_query[head] = jnp.dot(key_t[...], score_buf[head], preferred_element_type=F32)


def attend_back(
    low, high, key_pos, query, query_n, key, key_t, value, grad, grad_n, lse, delta
):
    heads, width, rows = query.shape
    tile = low_tile(rows)
    whole = lambda i: (0, 0)
    lane = lambda i: (0, i)
    wide = pl.BlockSpec((heads, width, tile), lambda i: (0, 0, i))
    tall = pl.BlockSpec((heads, tile, width), lambda i: (0, i, 0))
    row = pl.BlockSpec((heads, 1, tile), lambda i: (0, 0, i))
    keys = pl.BlockSpec((rows, width), whole)
    return pl.pallas_call(
        attend_back_kernel,
        grid=(rows // tile,),
        in_specs=[
            pl.BlockSpec((1, tile), lane),
            pl.BlockSpec((1, tile), lane),
            pl.BlockSpec((rows, tile), whole),
            wide, tall, keys, pl.BlockSpec((width, rows), whole), keys, wide, tall, row, row,
        ],
        out_specs=[wide, keys, keys],
        out_shape=[
            jax.ShapeDtypeStruct((heads, width, rows), F32),
            jax.ShapeDtypeStruct((rows, width), F32),
            jax.ShapeDtypeStruct((rows, width), F32),
        ],
        scratch_shapes=[pltpu.VMEM((heads, rows, tile), BF16)],
        cost_estimate=pl.CostEstimate(
            flops=10 * heads * rows * rows * 256,
            bytes_accessed=8 * rows * 256,
            transcendentals=heads * rows * rows,
        ),
        name="attend_back",
    )(low, high, key_pos, query, query_n, key, key_t, value, grad, grad_n, lse, delta)


def gather(values, name, axis=0):
    return lax.all_gather(values, name, axis=axis, tiled=True)


def exchange(values, name="expert"):
    return lax.all_to_all(values, name, split_axis=0, concat_axis=0, tiled=True)


def give_back(partial):
    return lax.psum_scatter(
        partial.astype(BF16), "expert", scatter_dimension=0, tiled=True
    ).astype(F32)


def local(
    hidden_in, d_out, gain_attn, w_qkv, w_o, gain_moe, w_router, w_in, w_out,
    seq_lengths, assign, routes,
):
    tok_rows, width = hidden_in.shape
    exp_dev, _, ff_two = w_in.shape
    ff = ff_two // 2
    n_expert = lax.axis_size("expert")
    me = lax.axis_index("expert")
    experts = exp_dev * n_expert
    group_rows = tok_rows * n_expert
    q_per = HEADS // n_expert
    share = GROUPS // q_per
    q_cols = q_per * HEAD_DIM
    k_base = HEADS * HEAD_DIM
    v_base = k_base + KV_HEADS * HEAD_DIM
    cols = q_cols + 2 * HEAD_DIM

    pack = gather(
        jnp.concatenate([gain_attn[None], gain_moe[None], w_router.T], axis=0), "dp", axis=1
    )
    gain_one, gain_two = pack[0].astype(F32), pack[1].astype(F32)
    router_t = pack[2:]
    kv_head = (me * q_per) // GROUPS
    w_heads = gather(
        jnp.concatenate(
            [
                lax.dynamic_slice_in_dim(w_qkv, me * q_cols, q_cols, 1),
                lax.dynamic_slice_in_dim(w_qkv, k_base + kv_head * HEAD_DIM, HEAD_DIM, 1),
                lax.dynamic_slice_in_dim(w_qkv, v_base + kv_head * HEAD_DIM, HEAD_DIM, 1),
            ],
            axis=1,
        ),
        "dp",
    )
    stream_in = hidden_in.astype(F32)
    normed_one = rms_norm(stream_in, gain_one).astype(BF16)
    normed_all = gather(normed_one, "expert")
    position = gather(assign[0], "expert")
    proj_full = gather(w_o, "dp")
    weight_in = gather(w_in, "dp", axis=1)
    d_out_all = gather(d_out, "expert")
    routes_all = gather(routes, "expert")
    weight_out = gather(w_out, "dp", axis=2)
    pieces = []
    for dev in range(n_expert):
        head = (dev * q_per) // GROUPS * HEAD_DIM
        pieces += [
            w_qkv[:, dev * q_cols : (dev + 1) * q_cols],
            w_qkv[:, k_base + head : k_base + head + HEAD_DIM],
            w_qkv[:, v_base + head : v_base + head + HEAD_DIM],
        ]
    qkv_full = gather(jnp.concatenate(pieces, axis=1), "dp")

    lengths = seq_lengths[0]
    ends = jnp.cumsum(lengths)
    starts = ends - lengths
    seq_id = jnp.sum((position[None, :] >= ends[:, None]).astype(jnp.int32), axis=0)
    picks = seq_id[None, :] == jnp.arange(lengths.shape[0], dtype=jnp.int32)[:, None]
    start_of = jnp.sum(jnp.where(picks, starts[:, None], 0), axis=0)
    rot_pos = position - start_of
    half = HEAD_DIM // 2
    frequency = ROPE_BASE ** (-(jnp.arange(half).astype(F32) * (2.0 / HEAD_DIM)))
    angles = frequency[:, None] * rot_pos.astype(F32)[None, :]
    cosine, sine = jnp.cos(angles), jnp.sin(angles)
    low, high = start_of[None, :], position[None, :]
    key_pos = jnp.broadcast_to(position[:, None], (group_rows, low_tile(group_rows)))

    projected = dot(w_heads, normed_all, 0, 1)
    query = jnp.stack(
        [
            rotate(projected[h * HEAD_DIM : (h + 1) * HEAD_DIM], cosine, sine).astype(BF16)
            for h in range(q_per)
        ]
    ) * jnp.asarray(SCORE_SCALE, BF16)
    key_t = rotate(projected[q_cols : q_cols + HEAD_DIM], cosine, sine).astype(BF16)
    value_t = projected[q_cols + HEAD_DIM :].astype(BF16)
    key, value = key_t.T, value_t.T
    heads_out, lse = attend(low, high, key_pos, query, key, value_t)
    attended_t = heads_out.reshape(q_cols, group_rows)
    attended = exchange(attended_t.T.reshape(n_expert, tok_rows, q_cols))
    attended = attended.transpose(1, 0, 2).reshape(tok_rows, HEADS * HEAD_DIM)
    mid_stream = stream_in + dot(attended, proj_full)
    normed_two = rms_norm(mid_stream, gain_two).astype(BF16)

    rows_all = gather(normed_two, "expert")
    named = jnp.any(
        routes_all[:, :, None] == jnp.arange(experts, dtype=jnp.int32)[None, None, :], axis=1
    )
    gates = jax.nn.softmax(jnp.where(named, dot(rows_all, router_t, 1, 1), -jnp.inf), axis=1)
    mine = lax.dynamic_slice_in_dim(gates, me * exp_dev, exp_dev, 1)
    made, d_rows, gate_cols, grads_in, grads_out = 0.0, 0.0, [], [], []
    for one in range(exp_dev):
        weight = mine[:, one : one + 1]
        d_plain = dot(d_out_all, weight_out[one], 1, 1)
        gate_up = dot(rows_all, weight_in[one])
        gate_pre, up_pre = gate_up[:, :ff], gate_up[:, ff:]
        sigmoid = jax.nn.sigmoid(gate_pre)
        active = gate_pre * sigmoid
        hidden = active * up_pre
        gate_cols.append(jnp.sum(hidden * d_plain, axis=1))
        scaled = (weight * hidden).astype(BF16)
        d_hidden = weight * d_plain
        d_gate_up = jnp.concatenate(
            [
                d_hidden * up_pre * sigmoid * (1.0 + gate_pre * (1.0 - sigmoid)),
                d_hidden * active,
            ],
            axis=1,
        ).astype(BF16)
        d_rows = d_rows + dot(d_gate_up, weight_in[one], 1, 1)
        made = made + dot(scaled, weight_out[one])
        grads_out.append(dot(scaled, d_out_all, 0, 0))
        grads_in.append(dot(rows_all, d_gate_up, 0, 0))
    d_gate = exchange(
        jnp.stack(gate_cols).reshape(exp_dev, n_expert, tok_rows).transpose(1, 0, 2)
    )
    d_gate = d_gate.reshape(experts, tok_rows).T
    d_back = give_back(d_rows)
    moe_sum = give_back(made)
    layer_out = (mid_stream + moe_sum).astype(BF16)
    grad_w_in = lax.psum_scatter(jnp.stack(grads_in), "dp", scatter_dimension=1, tiled=True)
    grad_w_out = lax.psum_scatter(jnp.stack(grads_out), "dp", scatter_dimension=2, tiled=True)

    own_gates = lax.dynamic_slice_in_dim(gates, me * tok_rows, tok_rows, 0)
    d_logits = (
        own_gates * (d_gate - jnp.sum(own_gates * d_gate, axis=1, keepdims=True))
    ).astype(BF16)
    grad_router = dot(d_logits, normed_two, 0, 0)
    d_normed_two = d_back + dot(d_logits, router_t)
    _, norm_two_back = jax.vjp(rms_norm, mid_stream, gain_two)
    d_mid_norm, grad_gain_two = norm_two_back(d_normed_two)
    d_mid = d_out.astype(F32) + d_mid_norm

    d_attn_all = gather(d_mid.astype(BF16), "expert")
    w_o_mine = lax.dynamic_slice_in_dim(proj_full, me * q_cols, q_cols, 0)
    d_heads = dot(w_o_mine, d_attn_all, 1, 1).astype(BF16).reshape(q_per, HEAD_DIM, group_rows)
    delta = jnp.sum(d_heads.astype(F32) * heads_out.astype(F32), axis=1, keepdims=True)
    d_query, d_key, d_value = attend_back(
        low, high, key_pos, query, jnp.swapaxes(query, 1, 2), key, key_t, value,
        d_heads, jnp.swapaxes(d_heads, 1, 2), lse, delta,
    )
    d_projected = jnp.concatenate(
        [rotate_back(d_query[h] * SCORE_SCALE, cosine, sine) for h in range(q_per)]
        + [rotate_back(d_key.T, cosine, sine), d_value.T],
        axis=0,
    ).astype(BF16)
    d_projected = d_projected.T
    d_own = exchange(d_projected.reshape(n_expert, tok_rows, cols))
    d_own = d_own.transpose(1, 0, 2).reshape(tok_rows, n_expert * cols)
    d_normed_one = dot(d_own, qkv_full, 1, 1)
    _, norm_one_back = jax.vjp(rms_norm, stream_in, gain_one)
    d_in_norm, grad_gain_one = norm_one_back(d_normed_one)
    grad_in = d_mid + d_in_norm

    part_o = lax.psum_scatter(
        dot(attended_t, d_attn_all), "dp", scatter_dimension=1, tiled=True
    )
    grad_w_o = lax.all_to_all(
        gather(part_o, "expert"), "dp", split_axis=0, concat_axis=1, tiled=True
    )
    part_qkv = lax.psum_scatter(
        dot(normed_all, d_projected, 0, 0), "dp", scatter_dimension=0, tiled=True
    )
    joined = lax.all_gather(part_qkv, "expert", axis=0)

    def columns(stack):
        return stack.transpose(1, 0, 2).reshape(stack.shape[1], -1)

    def shared(stack):
        return columns(stack.reshape((KV_HEADS, share) + stack.shape[1:]).sum(axis=1))

    grad_w_qkv = jnp.concatenate(
        [
            columns(joined[:, :, :q_cols]),
            shared(joined[:, :, q_cols : q_cols + HEAD_DIM]),
            shared(joined[:, :, q_cols + HEAD_DIM :]),
        ],
        axis=1,
    )
    small = jnp.concatenate([grad_gain_one[None], grad_gain_two[None], grad_router], axis=0)
    small = lax.psum(
        lax.psum_scatter(small, "dp", scatter_dimension=1, tiled=True), "expert"
    )
    return (
        layer_out, grad_in, small[0], grad_w_qkv, grad_w_o, small[1], small[2:].T,
        grad_w_in, grad_w_out,
    )


def solution(mesh):
    rows = P(("dp", "expert"), None)
    in_specs = (
        rows, rows, P("dp"), P("dp", None), P("dp", None), P("dp"), P("dp", None),
        P("expert", "dp", None), P("expert", None, "dp"), P("dp", None), P("dp", "expert"), rows,
    )
    out_specs = (
        rows, rows, P("dp"), P("dp", None), P("dp", None), P("dp"), P("dp", None),
        P("expert", "dp", None), P("expert", None, "dp"),
    )
    return jax.shard_map(local, mesh=mesh, in_specs=in_specs, out_specs=out_specs, check_vma=False)
```
